32 devices in a mesh: group: 4 (over x, core), batch: 8 (over z, y).
Axes of the slice: x: 2, y: 2, z: 4, core: 2. Of those that a mesh axis runs over, the one named last changes fastest.
Arguments:
- tokens: bfloat16 [32, 128, 1024], P('batch'), may hold values from -6 to 6
- memory: bfloat16 [32, 2048, 1024], P('batch'), may hold values from -6 to 6
- positions: int32 [32, 128], P('batch'), may hold values from 0 to 254, as said below
- norm_self: float32 [1024], replicated, may hold values from 0.25 to 1.75
- query_self: bfloat16 [1024, 1024], P(None, 'group'), may hold values from -0.25 to 0.25
- key_self: bfloat16 [1024, 512], P(None, 'group'), may hold values from -0.1875 to 0.1875
- value_self: bfloat16 [1024, 512], P(None, 'group'), may hold values from -0.1875 to 0.1875
- out_self: bfloat16 [1024, 1024], P('group'), may hold values from -1 to 1
- rel_bias: float32 [32, 16], P(None, 'group'), may hold values from -4 to 4
- norm_cross: float32 [1024], replicated, may hold values from 0.25 to 1.75
- query_cross: bfloat16 [1024, 1024], P(None, 'group'), may hold values from -0.25 to 0.25
- key_cross: bfloat16 [1024, 512], P(None, 'group'), may hold values from -0.1875 to 0.1875
- value_cross: bfloat16 [1024, 512], P(None, 'group'), may hold values from -0.1875 to 0.1875
- out_cross: bfloat16 [1024, 1024], P('group'), may hold values from -3 to 3
- norm_ffn: float32 [1024], replicated, may hold values from 0.25 to 1.75
- gate_in: bfloat16 [1024, 2816], P(None, 'group'), may hold values from -0.1875 to 0.1875
- up_in: bfloat16 [1024, 2816], P(None, 'group'), may hold values from -0.1875 to 0.1875
- down_proj: bfloat16 [2816, 1024], P('group'), may hold values from -0.4375 to 0.4375
- cotangent: bfloat16 [32, 128, 1024], P('batch'), may hold values from -6 to 6
Outputs:
- layer_out: float32 [32, 128, 1024], P('batch')
- grad_tokens: float32 [32, 128, 1024], P('batch')
- grad_memory: bfloat16 [32, 2048, 1024], P('batch')
- grad_norm_self: float32 [1024], replicated
- grad_query_self: float32 [1024, 1024], P(None, 'group')
- grad_key_self: float32 [1024, 512], P(None, 'group')
- grad_value_self: float32 [1024, 512], P(None, 'group')
- grad_out_self: float32 [1024, 1024], P('group')
- grad_rel_bias: float32 [32, 16], P(None, 'group')
- grad_norm_cross: float32 [1024], replicated
- grad_query_cross: float32 [1024, 1024], P(None, 'group')
- grad_key_cross: float32 [1024, 512], P(None, 'group')
- grad_value_cross: float32 [1024, 512], P(None, 'group')
- grad_out_cross: float32 [1024, 1024], P('group')
- grad_norm_ffn: float32 [1024], replicated
- grad_gate_in: float32 [1024, 2816], P(None, 'group')
- grad_up_in: float32 [1024, 2816], P(None, 'group')
- grad_down_proj: float32 [2816, 1024], P('group')
The draws below stay inside these ranges and needn't reach their ends.
Inputs may be any that keep to these rules, and one draw needn't show every extreme that they name: In each summary's row the positions start at 0 and rise by 1 or 2 from one token to the next; in the first summary they rise by 2 at every token.
All inputs are finite; a program needn't handle non-finite values.
Results may differ from the reference program's by a relative error of at most 0.025.
The reference program's roundings to bfloat16 on the way count: a program that leaves them out, or rounds other values in their place, can miss the bound.
Values may be sent and summed in bfloat16 or wider, within the bound.
No kernel may reach another device: no remote copies, remote signals or barrier semaphores. Data moves between devices by JAX's collectives and lax.ppermute only.
A program may use at most 256 MiB of HBM per device.

```python
import math
import jax
import jax.numpy as jnp
from jax import lax

D = 1024
H = 16
HD = 64
KV = 8
FF = 2816
NB = 32
MAXDIST = 128
TGT = 128
MEM = 2048
SEQS = 32


def draw_positions(key, part):
    steps = jax.random.randint(key, (SEQS, TGT), 1, 3, dtype=jnp.int32)
    first_row = (jnp.arange(SEQS, dtype=jnp.int32) == 0)[:, None]
    steps = jnp.where(first_row, jnp.int32(2), steps).astype(jnp.int32)
    return (jnp.cumsum(steps, axis=1) - steps[:, :1]).astype(jnp.int32)


def steps_of(rng, shape, cuts, least, high):
    def one(dim, parts):
        heights = jax.random.uniform(jax.random.fold_in(jax.random.fold_in(rng, 6), dim), (parts,), jnp.float32, least / len(cuts), high / len(cuts))
        return jnp.repeat(jnp.exp(heights), shape[dim] // parts).reshape((-1,) + (1,) * (len(shape) - dim - 1))

    level = one(*cuts[0])
    for cut in cuts[1:]:
        level = level * one(*cut)
    return level


def centred(own_key, shape, deviation, limit, cuts=(), kind=jnp.bfloat16):
    level = steps_of(own_key, shape, cuts, -0.22, 0.18) if cuts else 1.0
    values = jax.random.normal(own_key, shape, jnp.float32) * deviation * level
    return jnp.minimum(jnp.maximum(values, -limit), limit).astype(kind)


def setup_inputs(seed: int = 0) -> dict:
    key_list = jax.random.split(jax.random.key(seed), 20)
    return {
        "tokens": centred(key_list[0], (SEQS, TGT, D), 1.0, 6.0, ((0, 8),)),
        "memory": centred(key_list[1], (SEQS, MEM, D), 1.0, 6.0, ((0, 8),)),
        "positions": draw_positions(jax.random.fold_in(key_list[19], 71), 0),
        "norm_self": jnp.clip(1.0 + 0.15 * jax.random.normal(key_list[3], (D,), jnp.float32), 0.25, 1.75),
        "query_self": centred(key_list[4], (D, H * HD), (D // 2) ** -0.5, 0.25, ((1, 4),)),
        "key_self": centred(key_list[5], (D, KV * HD), D ** -0.5, 0.1875, ((1, 4),)),
        "value_self": centred(key_list[6], (D, KV * HD), D ** -0.5, 0.1875, ((1, 4),)),
        "out_self": centred(key_list[7], (H * HD, D), (max(H * HD // 32, 1)) ** -0.5, 1.0, ((0, 4),)),
        "rel_bias": centred(key_list[8], (NB, H), 1.0, 4.0, ((1, 4),), jnp.float32),
        "norm_cross": jnp.clip(1.0 + 0.15 * jax.random.normal(key_list[9], (D,), jnp.float32), 0.25, 1.75),
        "query_cross": centred(key_list[10], (D, H * HD), (D // 2) ** -0.5, 0.25, ((1, 4),)),
        "key_cross": centred(key_list[11], (D, KV * HD), D ** -0.5, 0.1875, ((1, 4),)),
        "value_cross": centred(key_list[12], (D, KV * HD), D ** -0.5, 0.1875, ((1, 4),)),
        "out_cross": centred(key_list[13], (H * HD, D), (max(H * HD // 256, 1)) ** -0.5, 3.0, ((0, 4),)),
        "norm_ffn": jnp.clip(1.0 + 0.15 * jax.random.normal(key_list[14], (D,), jnp.float32), 0.25, 1.75),
        "gate_in": centred(key_list[15], (D, FF), D ** -0.5, 0.1875, ((1, 4),)),
        "up_in": centred(key_list[16], (D, FF), D ** -0.5, 0.1875, ((1, 4),)),
        "down_proj": centred(key_list[17], (FF, D), (max(FF // 16, 1)) ** -0.5, 0.4375, ((0, 4),)),
        "cotangent": centred(key_list[18], (SEQS, TGT, D), 1.0, 6.0, ((0, 8),)),
    }


epsilon = 1e-06
masked_score = -1e+30
highest = lax.Precision.HIGHEST

@jax.custom_vjp
def low(v):
    return lax.optimization_barrier(v.astype(jnp.bfloat16)).astype(jnp.float32)

@jax.custom_vjp
def low_back(v):
    return v

def low_keep(v):
    return (low(v), None)

def low_pass(kept, grad):
    return (grad,)

def back_keep(v):
    return (v, None)

def back_low(kept, grad):
    return (low(grad),)
low.defvjp(low_keep, low_pass)
low_back.defvjp(back_keep, back_low)

def both_ways(value):
    return low(low_back(value))

def bucket_of(distance, levels, furthest):
    exact_span = levels // 2
    if distance < exact_span:
        return distance
    beyond = exact_span + math.floor(math.log(distance / exact_span) / math.log(furthest / exact_span) * (levels - exact_span))
    return min(beyond, levels - 1)

def bucket_bounds(levels, furthest):
    buckets = [bucket_of(distance, levels, furthest) for distance in range(furthest + 1)]
    return [sum((1 for value in buckets if value < rank_level)) for rank_level in range(1, levels)]

def bias_parts(positions, levels, furthest):
    bounds = jnp.asarray(bucket_bounds(levels, furthest), dtype=jnp.int32)
    distance = positions[:, :, None] - positions[:, None, :]
    bucket = lax.optimization_barrier(jnp.sum((distance[..., None] >= bounds).astype(jnp.int32), axis=-1)).astype(jnp.int32)
    onehot = (bucket[..., None] == jnp.arange(levels, dtype=jnp.int32)).astype(jnp.float32)
    return (onehot, distance >= 0)

def rms_norm(inputs, gain):
    return inputs * lax.rsqrt(lax.optimization_barrier(jnp.mean(inputs * inputs, axis=-1, keepdims=True)) + epsilon) * gain

def project(left, right):
    return jnp.einsum('std,de->ste', left, right, precision=highest)

def attend(queries, key_rows, value_rows, rel_terms, allowed, score_scale):
    scores = jnp.einsum('stkgd,sukd->skgtu', queries, key_rows, precision=highest) * score_scale
    if rel_terms is not None:
        scores = jnp.where(allowed, low_back(scores + rel_terms), masked_score)
    else:
        scores = low_back(scores)
    attn_probs = low(jax.nn.softmax(scores, axis=-1))
    return jnp.einsum('skgtu,sukd->stkgd', attn_probs, value_rows, precision=highest)

def layer(inputs, memory, norm_self, query_self, key_self, value_self, out_self, rel_bias, norm_cross, query_cross, key_cross, value_cross, out_cross, norm_ffn, gate_in, up_in, down_proj, onehot, allowed):
    seq_count, target_length, model_width = inputs.shape
    memory_length = memory.shape[1]
    share_count = H // KV
    score_scale = HD ** (-0.5)
    checked_attend = jax.checkpoint(attend)
    rel_terms = jnp.einsum('stub,bh->shtu', onehot, rel_bias, precision=highest)
    rel_terms = rel_terms.reshape(seq_count, KV, share_count, target_length, target_length)
    normed_one = low(rms_norm(inputs, norm_self))
    queries = both_ways(project(normed_one, query_self)).reshape(seq_count, target_length, KV, share_count, HD)
    keys_one = both_ways(project(normed_one, key_self)).reshape(seq_count, target_length, KV, HD)
    values_one = both_ways(project(normed_one, value_self)).reshape(seq_count, target_length, KV, HD)
    attended = checked_attend(queries, keys_one, values_one, rel_terms, allowed, score_scale)
    attended = both_ways(attended.reshape(seq_count, target_length, H * HD))
    hidden_one = inputs + low_back(project(attended, out_self))
    normed_two = low(rms_norm(hidden_one, norm_cross))
    queries_two = both_ways(project(normed_two, query_cross)).reshape(seq_count, target_length, KV, share_count, HD)
    keys_two = both_ways(project(memory, key_cross)).reshape(seq_count, memory_length, KV, HD)
    values_two = both_ways(project(memory, value_cross)).reshape(seq_count, memory_length, KV, HD)
    attended_two = checked_attend(queries_two, keys_two, values_two, None, None, score_scale)
    attended_two = both_ways(attended_two.reshape(seq_count, target_length, H * HD))
    hidden_two = hidden_one + low_back(project(attended_two, out_cross))
    normed_three = low(rms_norm(hidden_two, norm_ffn))
    gate_pre = low_back(project(normed_three, gate_in))
    up_pre = low_back(project(normed_three, up_in))
    hidden_units = low(jax.nn.gelu(gate_pre, approximate=True) * up_pre)
    return hidden_two + low_back(project(hidden_units, down_proj))

def reference(tokens, memory, positions, norm_self, query_self, key_self, value_self, out_self, rel_bias, norm_cross, query_cross, key_cross, value_cross, out_cross, norm_ffn, gate_in, up_in, down_proj, cotangent):
    onehot, allowed = bias_parts(positions, NB, MAXDIST)
    allowed = allowed[:, None, None]
    floats = (tokens.astype(jnp.float32), memory.astype(jnp.float32), norm_self, query_self.astype(jnp.float32), key_self.astype(jnp.float32), value_self.astype(jnp.float32), out_self.astype(jnp.float32), rel_bias, norm_cross, query_cross.astype(jnp.float32), key_cross.astype(jnp.float32), value_cross.astype(jnp.float32), out_cross.astype(jnp.float32), norm_ffn, gate_in.astype(jnp.float32), up_in.astype(jnp.float32), down_proj.astype(jnp.float32))

    def forward(*params):
        return layer(*params, onehot, allowed)
    layer_out, pull = jax.vjp(forward, *floats)
    grads = pull(cotangent.astype(jnp.float32))
    return (layer_out, grads[0], grads[1].astype(jnp.bfloat16), grads[2], grads[3], grads[4], grads[5], grads[6], grads[7], grads[8], grads[9], grads[10], grads[11], grads[12], grads[13], grads[14], grads[15], grads[16])
```

```python
import math

import jax
import jax.numpy as jnp
from jax import lax
from jax.experimental import pallas as pl
from jax.experimental.pallas import tpu as pltpu
from jax.sharding import PartitionSpec as P


HD = 64
NB = 32
MAXDIST = 128
LANES = 128
BLOCKS = 8

epsilon = 1e-06
masked_score = -1e30
score_scale = HD ** (-0.5)

BF = jnp.bfloat16
F32 = jnp.float32
NN = ((1,), (0,))
NT = ((1,), (1,))
TN = ((0,), (0,))


def bucket_of(distance, levels, furthest):
    exact_span = levels // 2
    if distance < exact_span:
        return distance
    beyond = exact_span + math.floor(
        math.log(distance / exact_span) / math.log(furthest / exact_span) * (levels - exact_span)
    )
    return min(beyond, levels - 1)


def bucket_bounds(levels, furthest):
    buckets = [bucket_of(distance, levels, furthest) for distance in range(furthest + 1)]
    return [sum((1 for value in buckets if value < rank_level)) for rank_level in range(1, levels)]


BOUNDS = bucket_bounds(NB, MAXDIST)


def dot(left, right, dims=NN):
    return lax.dot_general(left, right, (dims, ((), ())), preferred_element_type=F32)


def rms_scale(x):
    return lax.rsqrt(jnp.mean(x * x, axis=-1, keepdims=True) + epsilon)


def shape(dims, dtype):
    return jax.ShapeDtypeStruct(dims, dtype)


def call(body, grid, prefetch, ins, outs, scratch=(), flops=0, name=None):
    moved = sum(a.size * a.dtype.itemsize for a, _, _ in ins)
    moved += sum(math.prod(s) * jnp.dtype(d).itemsize for s, d, _, _ in outs)
    spec = pltpu.PrefetchScalarGridSpec(
        num_scalar_prefetch=1,
        grid=grid,
        in_specs=[
            pl.BlockSpec(memory_space=pltpu.SMEM) if block is None else pl.BlockSpec(block, index)
            for _, block, index in ins
        ],
        out_specs=[pl.BlockSpec(block, index) for _, _, block, index in outs],
        scratch_shapes=list(scratch),
    )
    return pl.pallas_call(
        body,
        grid_spec=spec,
        out_shape=[shape(s, d) for s, d, _, _ in outs],
        compiler_params=pltpu.CompilerParams(
            dimension_semantics=("arbitrary",) * len(grid), vmem_limit_bytes=56 << 20
        ),
        cost_estimate=pl.CostEstimate(flops=flops, transcendentals=0, bytes_accessed=moved),
        name=name,
    )(prefetch, *[a for a, _, _ in ins])


def fixed(rank):
    return lambda *_: (0,) * rank


def swap(x, axis, size, bit):
    return lax.ppermute(x, axis, [(i, i ^ bit) for i in range(size)])


def gather_group(x, group_size):
    far = swap(x, "group", group_size, 2)
    near = swap(x, "group", group_size, 1)
    both = swap(far, "group", group_size, 1)
    return (x, near, far, both)


def after(x, *others):
    return lax.optimization_barrier((x,) + others)[0]


class BatchSum:
    def __init__(self, batch_size, order):
        self.size = batch_size
        self.bits = [1 << k for k in order]
        total = batch_size.bit_length() - 1
        self.rest = [1 << k for k in range(total) if (1 << k) not in self.bits]
        me = lax.axis_index("batch")
        place = 0
        for k in order:
            place = place * 2 + ((me >> k) & 1)
        self.place = place

    def __call__(self, blocks):
        now = blocks
        for bit in self.bits:
            half = now.shape[0] // 2
            got = swap(now[half:].astype(BF), "batch", self.size, bit)
            now = now[:half].astype(F32) + got.astype(F32)
        for bit in self.rest:
            mine = now.astype(BF)
            now = mine.astype(F32) + swap(mine, "batch", self.size, bit).astype(F32)
        piece = now.astype(BF)
        for bit in self.bits[:0:-1]:
            piece = jnp.concatenate([piece, swap(piece, "batch", self.size, bit)], axis=0)
        return piece, swap(piece, "batch", self.size, self.bits[0])


def distance_of(column_ref, row_ref):
    return column_ref[0] - row_ref[0]


def self_forward(tokens, gain, weights, columns, rows, rel_bias, seqs, length, heads, groups):
    width = tokens.shape[1]
    total = weights.shape[1]
    share = heads // groups
    q_end, k_end = heads * HD, heads * HD + groups * HD

    def body(_, tok, g, w, col, row, rel, n1, qkv, probs, att):
        x = tok[...].astype(F32)
        normed = (x * rms_scale(x) * g[...]).astype(BF)
        n1[...] = normed
        proj = dot(normed, w[...]).astype(BF)
        qkv[...] = proj
        distance = distance_of(col, row)
        bias = [jnp.full((length, length), rel[0, h], F32) for h in range(heads)]
        for level, bound in enumerate(BOUNDS, start=1):
            reached = distance >= bound
            bias = [jnp.where(reached, rel[level, h], bias[h]) for h in range(heads)]
        allowed = distance >= 0
        parts = []
        for h in range(heads):
            kv = h // share
            q = proj[:, h * HD : (h + 1) * HD]
            k = proj[:, q_end + kv * HD : q_end + (kv + 1) * HD]
            v = proj[:, k_end + kv * HD : k_end + (kv + 1) * HD]
            scores = jnp.where(allowed, dot(q, k, NT) * score_scale + bias[h], masked_score)
            weight = jnp.exp(scores - jnp.max(scores, axis=-1, keepdims=True))
            p = weight / jnp.sum(weight, axis=-1, keepdims=True)
            probs[0, h] = p
            parts.append(dot(p.astype(BF), v))
        att[...] = jnp.concatenate(parts, axis=-1).astype(BF)

    return call(
        body,
        (seqs,),
        jnp.zeros((1,), jnp.int32),
        [
            (tokens, (length, width), lambda s, *_: (s, 0)),
            (gain, (1, width), fixed(2)),
            (weights, weights.shape, fixed(2)),
            (columns, (1, length, 1), lambda s, *_: (s, 0, 0)),
            (rows, (1, 1, length), lambda s, *_: (s, 0, 0)),
            (rel_bias, None, None),
        ],
        [
            ((seqs * length, width), BF, (length, width), lambda s, *_: (s, 0)),
            ((seqs * length, total), BF, (length, total), lambda s, *_: (s, 0)),
            (
                (seqs, heads, length, length),
                F32,
                (1, heads, length, length),
                lambda s, *_: (s, 0, 0, 0),
            ),
            ((seqs * length, heads * HD), BF, (length, heads * HD), lambda s, *_: (s, 0)),
        ],
        flops=2 * seqs * length * width * total,
        name="self_forward",
    )


def self_backward(qkv, probs, grad_att, columns, rows, seqs, length, heads, groups):
    total = qkv.shape[1]
    share = heads // groups
    q_end, k_end = heads * HD, heads * HD + groups * HD
    edges = [-(1 << 30)] + BOUNDS + [1 << 30]

    def body(_, proj_ref, probs_ref, da, col, row, dqkv, grel):
        proj = proj_ref[...]
        distance = distance_of(col, row)
        grads_q, grads_k, grads_v, kept = [], [], [], []
        for h in range(heads):
            kv = h // share
            q = proj[:, h * HD : (h + 1) * HD]
            k = proj[:, q_end + kv * HD : q_end + (kv + 1) * HD]
            v = proj[:, k_end + kv * HD : k_end + (kv + 1) * HD]
            d = da[:, h * HD : (h + 1) * HD]
            p = probs_ref[0, h]
            dp = dot(d, v, NT)
            ds = (p * (dp - jnp.sum(dp * p, axis=-1, keepdims=True))).astype(BF)
            kept.append(ds.astype(F32))
            grads_q.append(dot(ds, k) * score_scale)
            dk = dot(ds, q, TN) * score_scale
            dv = dot(p.astype(BF), d, TN)
            if h % share:
                grads_k[kv] = grads_k[kv] + dk
                grads_v[kv] = grads_v[kv] + dv
            else:
                grads_k.append(dk)
                grads_v.append(dv)
        dqkv[...] = jnp.concatenate(grads_q + grads_k + grads_v, axis=-1).astype(BF)
        for level in range(NB):
            inside = jnp.logical_and(distance >= edges[level], distance < edges[level + 1])
            for h in range(heads):
                grel[0, level : level + 1, h * length : (h + 1) * length] = jnp.sum(
                    jnp.where(inside, kept[h], 0.0), axis=0, keepdims=True
                )

    return call(
        body,
        (seqs,),
        jnp.zeros((1,), jnp.int32),
        [
            (qkv, (length, total), lambda s, *_: (s, 0)),
            (probs, (1, heads, length, length), lambda s, *_: (s, 0, 0, 0)),
            (grad_att, (length, heads * HD), lambda s, *_: (s, 0)),
            (columns, (1, length, 1), lambda s, *_: (s, 0, 0)),
            (rows, (1, 1, length), lambda s, *_: (s, 0, 0)),
        ],
        [
            ((seqs * length, total), BF, (length, total), lambda s, *_: (s, 0)),
            (
                (seqs, NB, heads * length),
                F32,
                (1, NB, heads * length),
                lambda s, *_: (s, 0, 0),
            ),
        ],
        flops=10 * seqs * heads * length * length * HD,
        name="self_backward",
    )


def stack_heads(x, heads, groups):
    share = heads // groups
    zero = jnp.zeros((x.shape[0], HD), x.dtype)
    out = []
    for h in range(heads):
        own = x[:, h * HD : (h + 1) * HD]
        out.append(
            jnp.concatenate([own if g == h // share else zero for g in range(groups)], axis=-1)
        )
    return jnp.concatenate(out, axis=0)


def unstack_heads(x, heads, groups, length):
    share = heads // groups
    return jnp.concatenate(
        [
            x[(h // share) * HD : (h // share + 1) * HD, h * length : (h + 1) * length]
            for h in range(heads)
        ],
        axis=0,
    ).T


CHUNK = 256


def cross_forward(queries, kv, seqs, length, mem, heads, groups):
    wide = heads * length
    gw = groups * HD
    chunks = mem // CHUNK

    def body(_, q, kv_ref, att, lse, scores, acc):
        stacked = stack_heads(q[...], heads, groups) * jnp.asarray(score_scale, BF)

        def first(c, top):
            at = pl.ds(pl.multiple_of(c * CHUNK, CHUNK), CHUNK)
            s = dot(kv_ref[at, 0:gw], stacked, NT)
            scores[at, :] = s
            return jnp.maximum(top, jnp.max(s.reshape(CHUNK // 8, 8, wide), axis=0))

        top = lax.fori_loop(0, chunks, first, jnp.full((8, wide), -jnp.inf, F32))
        top = jnp.max(top, axis=0, keepdims=True)

        def second(c, total):
            at = pl.ds(pl.multiple_of(c * CHUNK, CHUNK), CHUNK)
            e = jnp.exp(scores[at, :] - top)
            scores[at, :] = e
            return total + jnp.sum(e.reshape(CHUNK // 8, 8, wide), axis=0)

        total = lax.fori_loop(0, chunks, second, jnp.zeros((8, wide), F32))
        total = jnp.sum(total, axis=0, keepdims=True)
        inverse = 1.0 / total
        lse[0] = top + jnp.log(total)
        acc[...] = jnp.zeros_like(acc)

        def third(c, carry):
            at = pl.ds(pl.multiple_of(c * CHUNK, CHUNK), CHUNK)
            p = (scores[at, :] * inverse).astype(BF)
            acc[...] += dot(kv_ref[at, gw : 2 * gw], p, TN)
            return carry

        lax.fori_loop(0, chunks, third, 0)
        att[...] = unstack_heads(acc[...], heads, groups, length).astype(BF)

    return call(
        body,
        (seqs,),
        jnp.zeros((1,), jnp.int32),
        [
            (queries, (length, heads * HD), lambda s, *_: (s, 0)),
            (kv, (mem, 2 * gw), lambda s, *_: (s, 0)),
        ],
        [
            ((seqs * length, heads * HD), BF, (length, heads * HD), lambda s, *_: (s, 0)),
            ((seqs, 1, wide), F32, (1, 1, wide), lambda s, *_: (s, 0, 0)),
        ],
        scratch=[pltpu.VMEM((mem, wide), F32), pltpu.VMEM((gw, wide), F32)],
        flops=8 * 4 * seqs * mem * wide * gw,
        name="cross_forward",
    )


def cross_backward(queries, kv, grad_att, lse, seqs, length, mem, heads, groups):
    wide = heads * length
    gw = groups * HD
    chunks = mem // CHUNK

    def body(_, q, kv_ref, da, lse_ref, dq, dkv, probs, gprobs, acc):
        stacked = stack_heads(q[...], heads, groups) * jnp.asarray(score_scale, BF)
        grads = stack_heads(da[...], heads, groups)
        level = lse_ref[0]

        def first(c, inner):
            at = pl.ds(pl.multiple_of(c * CHUNK, CHUNK), CHUNK)
            p = jnp.exp(dot(kv_ref[at, 0:gw], stacked, NT) - level)
            dp = dot(kv_ref[at, gw : 2 * gw], grads, NT)
            probs[at, :] = p
            gprobs[at, :] = dp
            dkv[at, gw : 2 * gw] = dot(p.astype(BF), grads).astype(BF)
            return inner + jnp.sum((p * dp).reshape(CHUNK // 8, 8, wide), axis=0)

        inner = lax.fori_loop(0, chunks, first, jnp.zeros((8, wide), F32))
        inner = jnp.sum(inner, axis=0, keepdims=True)
        acc[...] = jnp.zeros_like(acc)

        def second(c, carry):
            at = pl.ds(pl.multiple_of(c * CHUNK, CHUNK), CHUNK)
            ds = (probs[at, :] * (gprobs[at, :] - inner)).astype(BF)
            dkv[at, 0:gw] = dot(ds, stacked).astype(BF)
            acc[...] += dot(kv_ref[at, 0:gw], ds, TN)
            return carry

        lax.fori_loop(0, chunks, second, 0)
        dq[...] = (unstack_heads(acc[...], heads, groups, length) * score_scale).astype(BF)

    return call(
        body,
        (seqs,),
        jnp.zeros((1,), jnp.int32),
        [
            (queries, (length, heads * HD), lambda s, *_: (s, 0)),
            (kv, (mem, 2 * gw), lambda s, *_: (s, 0)),
            (grad_att, (length, heads * HD), lambda s, *_: (s, 0)),
            (lse, (1, 1, wide), lambda s, *_: (s, 0, 0)),
        ],
        [
            ((seqs * length, heads * HD), BF, (length, heads * HD), lambda s, *_: (s, 0)),
            ((seqs * mem, 2 * gw), BF, (mem, 2 * gw), lambda s, *_: (s, 0)),
        ],
        scratch=[
            pltpu.VMEM((mem, wide), F32),
            pltpu.VMEM((mem, wide), F32),
            pltpu.VMEM((gw, wide), F32),
        ],
        flops=8 * 10 * seqs * mem * wide * gw,
        name="cross_backward",
    )


TILE = 128


def joined(me, pieces, store, weights, dims):
    for r, piece in enumerate(pieces):
        store[r] = piece[...]
    out = None
    for j in range(4):
        at = j ^ me
        part = dot(store[at], weights[at], dims)
        out = part if out is None else out + part
    return out


def row_blocks(array):
    return (array, (TILE, array.shape[1]), lambda i, *_: (i, 0))


def whole(array):
    return (array, array.shape, fixed(array.ndim))


def out_rows(rows, cols, dtype):
    return ((rows, cols), dtype, (TILE, cols), lambda i, *_: (i, 0))


def join_self(me, pieces, weights, tokens, gain, wq):
    rows, width = tokens.shape
    k = pieces[0].shape[1]

    def body(me_ref, p0, p1, p2, p3, w, tok, g, wq_ref, x1, n2, q2, store):
        x = tok[...].astype(F32) + joined(me_ref[0], (p0, p1, p2, p3), store, w, NN)
        x1[...] = x
        normed = (x * rms_scale(x) * g[...]).astype(BF)
        n2[...] = normed
        q2[...] = dot(normed, wq_ref[...]).astype(BF)

    return call(
        body,
        (rows // TILE,),
        me,
        [row_blocks(p) for p in pieces]
        + [whole(weights), row_blocks(tokens), whole(gain), whole(wq)],
        [
            out_rows(rows, width, F32),
            out_rows(rows, width, BF),
            out_rows(rows, wq.shape[1], BF),
        ],
        scratch=[pltpu.VMEM((4, TILE, k), BF)],
        flops=2 * rows * width * (4 * k + wq.shape[1]),
        name="join_self",
    )


def feed_forward(me, pieces, weights, x1, gain, gate_in, up_in, down, cot):
    rows, width = x1.shape
    k = pieces[0].shape[1]
    units = gate_in.shape[1]
    half = rows // 2
    per_half = half // TILE
    root = math.sqrt(2.0 / math.pi)

    def body(
        me_ref, p0, p1, p2, p3, w, x1_ref, g, wg, wu, wd, cot_ref,
        x2, n3, hid, dgate, dup, branch, dn3, store,
    ):
        x = x1_ref[...] + joined(me_ref[0], (p0, p1, p2, p3), store, w, NN)
        x2[...] = x
        normed = (x * rms_scale(x) * g[...]).astype(BF)
        n3[...] = normed
        gate = dot(normed, wg[...])
        up = dot(normed, wu[...])
        square = gate * gate
        t = jnp.tanh(root * (gate + 0.044715 * (square * gate)))
        cdf = 0.5 * (1.0 + t)
        act = gate * cdf
        hidden = (act * up).astype(BF)
        hid[...] = hidden
        slope = cdf + 0.5 * gate * (1.0 - t * t) * (root * (1.0 + 3 * 0.044715 * square))
        dh = dot(cot_ref[...], wd[...], NT)
        dg = (dh * up * slope).astype(BF)
        du = (dh * act).astype(BF)
        dgate[...] = dg
        dup[...] = du
        dn3[0] = dot(dg, wg[...], NT) + dot(du, wu[...], NT)
        branch[0] = dot(hidden, wd[...])

    def half_map(i, me_ref):
        return ((i // per_half) ^ (me_ref[0] & 1), i % per_half, 0)

    halves = ((2, half, width), F32, (1, TILE, width), half_map)
    return call(
        body,
        (rows // TILE,),
        me,
        [row_blocks(p) for p in pieces]
        + [
            whole(weights),
            row_blocks(x1),
            whole(gain),
            whole(gate_in),
            whole(up_in),
            whole(down),
            row_blocks(cot),
        ],
        [
            out_rows(rows, width, F32),
            out_rows(rows, width, BF),
            out_rows(rows, units, BF),
            out_rows(rows, units, BF),
            out_rows(rows, units, BF),
            halves,
            halves,
        ],
        scratch=[pltpu.VMEM((4, TILE, k), BF)],
        flops=2 * rows * width * (4 * k + 6 * units),
        name="feed_forward",
    )


def norm_pull(x, gain, dn, base):
    r = rms_scale(x)
    c = dn * gain
    grad = base + r * c - x * ((r * r * r) * jnp.mean(c * x, axis=-1, keepdims=True))
    return grad, jnp.sum(dn * x * r, axis=0, keepdims=True)


def accumulate(ref, value):
    @pl.when(pl.program_id(0) == 0)
    def _():
        ref[...] = value

    @pl.when(pl.program_id(0) > 0)
    def _():
        ref[...] += value


def gain_out(width):
    return ((1, width), F32, (1, width), fixed(2))


def half_blocks(array, per_half):
    return (array, (TILE, array.shape[1]), lambda i, *_: (i % per_half, 0))


def pull_ffn(me, own, other, x2, gain, cot, wout):
    rows, width = x2.shape
    per_half = own.shape[0] // TILE

    def body(me_ref, a, b, x_ref, g, cot_ref, w, dx, e, da, gn):
        mine = (pl.program_id(0) // per_half) == (me_ref[0] & 1)
        dn = jnp.where(mine, a[...], b[...])
        grad, gsum = norm_pull(x_ref[...], g[...], dn, cot_ref[...].astype(F32))
        dx[...] = grad
        low = grad.astype(BF)
        e[...] = low
        da[...] = dot(low, w[...], NT).astype(BF)
        accumulate(gn, gsum)

    return call(
        body,
        (rows // TILE,),
        me,
        [
            half_blocks(own, per_half),
            half_blocks(other, per_half),
            row_blocks(x2),
            whole(gain),
            row_blocks(cot),
            whole(wout),
        ],
        [
            out_rows(rows, width, F32),
            out_rows(rows, width, BF),
            out_rows(rows, wout.shape[0], BF),
            gain_out(width),
        ],
        flops=2 * rows * width * wout.shape[0],
        name="pull_ffn",
    )


def finish_layer(me, own, other, x2):
    rows, width = x2.shape
    per_half = own.shape[0] // TILE

    def body(me_ref, a, b, x_ref, out):
        mine = (pl.program_id(0) // per_half) == (me_ref[0] & 1)
        out[...] = x_ref[...] + jnp.where(mine, a[...], b[...])

    return call(
        body,
        (rows // TILE,),
        me,
        [half_blocks(own, per_half), half_blocks(other, per_half), row_blocks(x2)],
        [out_rows(rows, width, F32)],
        name="finish_layer",
    )[0]


def pull_cross(me, pieces, weights, x1, gain, base, wout):
    rows, width = x1.shape
    k = pieces[0].shape[1]

    def body(me_ref, p0, p1, p2, p3, w, x_ref, g, base_ref, wo, dx, e, da, gn, store):
        dn = joined(me_ref[0], (p0, p1, p2, p3), store, w, NT)
        grad, gsum = norm_pull(x_ref[...], g[...], dn, base_ref[...])
        dx[...] = grad
        low = grad.astype(BF)
        e[...] = low
        da[...] = dot(low, wo[...], NT).astype(BF)
        accumulate(gn, gsum)

    return call(
        body,
        (rows // TILE,),
        me,
        [row_blocks(p) for p in pieces]
        + [whole(weights), row_blocks(x1), whole(gain), row_blocks(base), whole(wout)],
        [
            out_rows(rows, width, F32),
            out_rows(rows, width, BF),
            out_rows(rows, wout.shape[0], BF),
            gain_out(width),
        ],
        scratch=[pltpu.VMEM((4, TILE, k), BF)],
        flops=2 * rows * width * (4 * k + wout.shape[0]),
        name="pull_cross",
    )


def pull_self(me, pieces, weights, tokens, gain, base):
    rows, width = tokens.shape
    k = pieces[0].shape[1]

    def body(me_ref, p0, p1, p2, p3, w, x_ref, g, base_ref, dx, gn, store):
        dn = joined(me_ref[0], (p0, p1, p2, p3), store, w, NT)
        grad, gsum = norm_pull(x_ref[...].astype(F32), g[...], dn, base_ref[...])
        dx[...] = grad
        accumulate(gn, gsum)

    return call(
        body,
        (rows // TILE,),
        me,
        [row_blocks(p) for p in pieces]
        + [whole(weights), row_blocks(tokens), whole(gain), row_blocks(base)],
        [out_rows(rows, width, F32), gain_out(width)],
        scratch=[pltpu.VMEM((4, TILE, k), BF)],
        flops=2 * rows * width * 4 * k,
        name="pull_self",
    )


def memory_grad(me, pieces, weights):
    rows, k = pieces[0].shape
    width = weights.shape[1]
    tile = 512

    def body(me_ref, p0, p1, p2, p3, w, out, store):
        out[...] = joined(me_ref[0], (p0, p1, p2, p3), store, w, NT).astype(BF)

    return call(
        body,
        (rows // tile,),
        me,
        [(p, (tile, k), lambda i, *_: (i, 0)) for p in pieces] + [whole(weights)],
        [((rows, width), BF, (tile, width), lambda i, *_: (i, 0))],
        scratch=[pltpu.VMEM((4, tile, k), BF)],
        flops=2 * rows * width * 4 * k,
        name="memory_grad",
    )[0]


def grad_rows(place, left, rights):
    rows, width = left.shape
    part = width // BLOCKS

    def body(_, a, *refs):
        for b, out in zip(refs[: len(rights)], refs[len(rights) :]):
            out[0] = dot(a[...], b[...], TN).astype(BF)

    return call(
        body,
        (BLOCKS,),
        place,
        [(left, (rows, part), lambda j, *_: (0, j))] + [whole(r) for r in rights],
        [
            (
                (BLOCKS, part, r.shape[1]),
                BF,
                (1, part, r.shape[1]),
                lambda j, place_ref: (j ^ place_ref[0], 0, 0),
            )
            for r in rights
        ],
        flops=2 * rows * width * sum(r.shape[1] for r in rights),
        name="grad_rows",
    )


def grad_cols(place, left, right):
    rows, width = right.shape
    part = width // BLOCKS
    high = left.shape[1]

    def body(_, a, b, out):
        out[0] = dot(a[...], b[...], TN).astype(BF)

    return call(
        body,
        (BLOCKS,),
        place,
        [whole(left), (right, (rows, part), lambda j, *_: (0, j))],
        [
            (
                (BLOCKS, high, part),
                BF,
                (1, high, part),
                lambda j, place_ref: (j ^ place_ref[0], 0, 0),
            )
        ],
        flops=2 * rows * width * high,
        name="grad_cols",
    )[0]


def grad_memory_weights(place, dkv, memory):
    rows, width = memory.shape
    high = dkv.shape[1]
    part = width // BLOCKS
    step = 1024

    def body(place_ref, a, b, out, acc):
        value = dot(a[...], b[...], TN)

        @pl.when(pl.program_id(0) == 0)
        def _():
            acc[...] = value

        @pl.when(pl.program_id(0) > 0)
        def _():
            acc[...] += value

        @pl.when(pl.program_id(0) == pl.num_programs(0) - 1)
        def _():
            for j in range(BLOCKS):
                out[j ^ place_ref[0]] = acc[:, j * part : (j + 1) * part].astype(BF)

    return call(
        body,
        (rows // step,),
        place,
        [
            (dkv, (step, high), lambda i, *_: (i, 0)),
            (memory, (step, width), lambda i, *_: (i, 0)),
        ],
        [((BLOCKS, high, part), BF, (BLOCKS, high, part), fixed(3))],
        scratch=[pltpu.VMEM((high, width), F32)],
        flops=2 * rows * width * high,
        name="grad_memory_weights",
    )[0]


def restore(place, low, high, kind, widths=None):
    count = low.shape[0]
    _, a, b = low.shape
    widths = widths or [b]

    def body(place_ref, lo, hi, *outs):
        at = pl.program_id(0) ^ place_ref[0]
        value = jnp.where(at < count, lo[0].astype(F32), hi[0].astype(F32))
        if kind == "turned":
            value = value.T
        start = 0
        for out, w in zip(outs, widths):
            out[...] = value[:, start : start + w] if len(widths) > 1 else value
            start += w

    def block_map(j, place_ref):
        return ((j ^ place_ref[0]) & (count - 1), 0, 0)

    if kind == "rows":
        outs = [
            ((BLOCKS * a, w), F32, (a, w), lambda j, *_: (j, 0)) for w in widths
        ]
    elif kind == "turned":
        outs = [
            ((BLOCKS * b, w), F32, (b, w), lambda j, *_: (j, 0)) for w in widths
        ]
    else:
        outs = [((a, BLOCKS * b), F32, (a, b), lambda j, *_: (0, j))]
    return call(
        body,
        (BLOCKS,),
        place,
        [(low, (1, a, b), block_map), (high, (1, a, b), block_map)],
        outs,
        name="restore",
    )


def on_device(
    group_size,
    batch_size,
    tokens,
    memory,
    positions,
    norm_self,
    query_self,
    key_self,
    value_self,
    out_self,
    rel_bias,
    norm_cross,
    query_cross,
    key_cross,
    value_cross,
    out_cross,
    norm_ffn,
    gate_in,
    up_in,
    down_proj,
    cotangent,
):
    seqs, length, width = tokens.shape
    mem = memory.shape[1]
    groups = key_self.shape[1] // HD
    heads = query_self.shape[1] // HD
    group_index = lax.axis_index("group").astype(jnp.int32)
    me = group_index[None]
    along_y = BatchSum(batch_size, (0, 1, 2))
    along_z = BatchSum(batch_size, (1, 2, 0))
    place_y = along_y.place.astype(jnp.int32)[None]
    place_z = along_z.place.astype(jnp.int32)[None]

    tok = tokens.reshape(seqs * length, width)
    cot = cotangent.reshape(seqs * length, width)
    mem_rows = memory.reshape(seqs * mem, width)
    columns = positions[:, :, None]
    rows = positions[:, None, :]
    gain_self, gain_cross, gain_ffn = norm_self[None], norm_cross[None], norm_ffn[None]
    w_self = jnp.concatenate([query_self, key_self, value_self], axis=1)
    w_mem = jnp.concatenate([key_cross, value_cross], axis=1)

    def gather_weight(w):
        return jnp.stack(gather_group(w, group_size))

    all_out_self = gather_weight(out_self)
    n1, qkv, probs, a1 = self_forward(
        tok, gain_self, w_self, columns, rows, rel_bias, seqs, length, heads, groups
    )
    a1_all = gather_group(a1, group_size)
    kv = dot(mem_rows, w_mem).astype(BF)
    all_out_cross = gather_weight(after(out_cross, a1_all[2]))
    x1, n2, q2 = join_self(me, a1_all, all_out_self, tok, gain_cross, query_cross)
    all_query_cross = gather_weight(after(query_cross, q2))
    a2, lse = cross_forward(q2, kv, seqs, length, mem, heads, groups)
    a2_all = gather_group(a2, group_size)
    x2, n3, hidden, dgate, dup, branch, dn3 = feed_forward(
        me, a2_all, all_out_cross, x1, gain_ffn, gate_in, up_in, down_proj, cot
    )

    def sum_group(halves):
        got = swap(halves[1], "group", group_size, 1)
        mine = (halves[0] + got).astype(BF)
        full = mine.astype(F32) + swap(mine, "group", group_size, 2).astype(F32)
        return full, swap(full, "group", group_size, 1)

    dn3_own, dn3_other = sum_group(dn3)
    grad_gate_b, grad_up_b = grad_rows(place_y, n3, [dgate, dup])
    grad_down_b = grad_cols(place_z, hidden, cot)
    gate_sum = along_y(grad_gate_b)
    up_sum = along_y(grad_up_b)
    down_sum = along_z(grad_down_b)

    dx2, e2, da2, gn_ffn = pull_ffn(me, dn3_own, dn3_other, x2, gain_ffn, cot, out_cross)
    branch_own, branch_other = sum_group(after(branch, da2))
    layer_out = finish_layer(me, branch_own, branch_other, x2)
    all_self = gather_weight(after(w_self, da2))
    all_mem = gather_weight(after(w_mem, da2))

    dq2, dkv = cross_backward(q2, kv, da2, lse, seqs, length, mem, heads, groups)
    dq2_all = gather_group(dq2, group_size)
    parts = []
    for s in range(seqs):
        piece = after(dkv[s * mem : (s + 1) * mem], dq2_all[2])
        parts.append(gather_group(piece, group_size))
    dx1, e1, da1, gn_cross = pull_cross(
        me, dq2_all, all_query_cross, x1, gain_cross, dx2, out_self
    )
    grad_out_cross_b = grad_cols(place_z, a2, e2)
    grad_query_cross_b = grad_rows(place_y, n2, [dq2])[0]
    grad_kv_b = grad_memory_weights(place_y, dkv, mem_rows)
    out_cross_sum = along_z(grad_out_cross_b)
    query_cross_sum = along_y(grad_query_cross_b)
    kv_sum = along_y(grad_kv_b)

    dqkv, grel = self_backward(qkv, probs, da1, columns, rows, seqs, length, heads, groups)
    dqkv_all = gather_group(dqkv, group_size)
    grad_self_b = grad_rows(place_y, n1, [dqkv])[0]
    grad_out_self_b = grad_cols(place_z, a1, e1)
    self_sum = along_y(grad_self_b)
    out_self_sum = along_z(grad_out_self_b)
    grad_tokens, gn_self = pull_self(me, dqkv_all, all_self, tok, gain_self, dx1)

    grel = jnp.sum(grel.reshape(seqs, NB, heads, length), axis=(0, 3))
    small = jnp.concatenate([gn_self, gn_cross, gn_ffn, grel.reshape(1, -1)], axis=1)
    bit = 1
    while bit < batch_size:
        small = small + swap(small, "batch", batch_size, bit)
        bit *= 2

    grad_memory = jnp.stack([memory_grad(me, p, all_mem) for p in parts])

    q_width, k_width = heads * HD, groups * HD
    grad_query_self, grad_key_self, grad_value_self = restore(
        place_y, *self_sum, "rows", [q_width, k_width, k_width]
    )
    grad_out_self = restore(place_z, *out_self_sum, "cols")[0]
    grad_query_cross = restore(place_y, *query_cross_sum, "rows")[0]
    grad_key_cross, grad_value_cross = restore(place_y, *kv_sum, "turned", [k_width, k_width])
    grad_out_cross = restore(place_z, *out_cross_sum, "cols")[0]
    grad_gate = restore(place_y, *gate_sum, "rows")[0]
    grad_up = restore(place_y, *up_sum, "rows")[0]
    grad_down = restore(place_z, *down_sum, "cols")[0]

    flat = small[0]
    return (
        layer_out.reshape(seqs, length, width),
        grad_tokens.reshape(seqs, length, width),
        grad_memory,
        flat[:width],
        grad_query_self,
        grad_key_self,
        grad_value_self,
        grad_out_self,
        flat[3 * width :].reshape(NB, heads),
        flat[width : 2 * width],
        grad_query_cross,
        grad_key_cross,
        grad_value_cross,
        grad_out_cross,
        flat[2 * width : 3 * width],
        grad_gate,
        grad_up,
        grad_down,
    )


def solution(mesh):
    placed = (
        P("batch", None, None),
        P("batch", None, None),
        P("batch", None),
        P(),
        P(None, "group"),
        P(None, "group"),
        P(None, "group"),
        P("group", None),
        P(None, "group"),
        P(),
        P(None, "group"),
        P(None, "group"),
        P(None, "group"),
        P("group", None),
        P(),
        P(None, "group"),
        P(None, "group"),
        P("group", None),
        P("batch", None, None),
    )
    group_size = mesh.shape["group"]
    batch_size = mesh.shape["batch"]

    def run(*args):
        return on_device(group_size, batch_size, *args)

    return jax.shard_map(
        run,
        mesh=mesh,
        in_specs=placed,
        out_specs=(
            P("batch", None, None),
            P("batch", None, None),
            P("batch", None, None),
            P(),
            P(None, "group"),
            P(None, "group"),
            P(None, "group"),
            P("group", None),
            P(None, "group"),
            P(),
            P(None, "group"),
            P(None, "group"),
            P(None, "group"),
            P("group", None),
            P(),
            P(None, "group"),
            P(None, "group"),
            P("group", None),
        ),
        check_vma=False,
    )
```

```python
import math

import jax
import jax.numpy as jnp
from jax import lax
from jax.experimental import pallas as pl
from jax.experimental.pallas import tpu as pltpu
from jax.sharding import PartitionSpec as P


HD = 64
NB = 32
MAXDIST = 128
LANES = 128
BLOCKS = 8

epsilon = 1e-06
masked_score = -1e30
score_scale = HD ** (-0.5)

BF = jnp.bfloat16
F32 = jnp.float32
NN = ((1,), (0,))
NT = ((1,), (1,))
TN = ((0,), (0,))


def bucket_of(distance, levels, furthest):
    exact_span = levels // 2
    if distance < exact_span:
        return distance
    beyond = exact_span + math.floor(
        math.log(distance / exact_span) / math.log(furthest / exact_span) * (levels - exact_span)
    )
    return min(beyond, levels - 1)


def bucket_bounds(levels, furthest):
    buckets = [bucket_of(distance, levels, furthest) for distance in range(furthest + 1)]
    return [sum((1 for value in buckets if value < rank_level)) for rank_level in range(1, levels)]


BOUNDS = bucket_bounds(NB, MAXDIST)


def dot(left, right, dims=NN):
    return lax.dot_general(left, right, (dims, ((), ())), preferred_element_type=F32)


def rms_scale(x):
    return lax.rsqrt(jnp.mean(x * x, axis=-1, keepdims=True) + epsilon)


def shape(dims, dtype):
    return jax.ShapeDtypeStruct(dims, dtype)


def call(body, grid, prefetch, ins, outs, scratch=(), flops=0, name=None, onto=None):
    moved = sum(a.size * a.dtype.itemsize for a, _, _ in ins)
    moved += sum(math.prod(s) * jnp.dtype(d).itemsize for s, d, _, _ in outs)
    spec = pltpu.PrefetchScalarGridSpec(
        num_scalar_prefetch=1,
        grid=grid,
        in_specs=[
            pl.BlockSpec(memory_space=pltpu.SMEM) if block is None else pl.BlockSpec(block, index)
            for _, block, index in ins
        ]
        + ([] if onto is None else [pl.BlockSpec(memory_space=pl.ANY)]),
        out_specs=[pl.BlockSpec(block, index) for _, _, block, index in outs],
        scratch_shapes=list(scratch),
    )
    return pl.pallas_call(
        body,
        grid_spec=spec,
        out_shape=[shape(s, d) for s, d, _, _ in outs],
        compiler_params=pltpu.CompilerParams(
            dimension_semantics=("arbitrary",) * len(grid), vmem_limit_bytes=56 << 20
        ),
        cost_estimate=pl.CostEstimate(flops=flops, transcendentals=0, bytes_accessed=moved),
        input_output_aliases={} if onto is None else {1 + len(ins): 0},
        name=name,
    )(prefetch, *[a for a, _, _ in ins], *(() if onto is None else (onto,)))


def fixed(rank):
    return lambda *_: (0,) * rank


def swap(x, axis, size, bit):
    return lax.ppermute(x, axis, [(i, i ^ bit) for i in range(size)])


def gather_group(x, group_size):
    far = swap(x, "group", group_size, 2)
    near = swap(x, "group", group_size, 1)
    both = swap(far, "group", group_size, 1)
    return (x, near, far, both)


def after(x, *others):
    return lax.optimization_barrier((x,) + others)[0]


class BatchSum:
    def __init__(self, batch_size, order):
        self.size = batch_size
        self.bits = [1 << k for k in order]
        total = batch_size.bit_length() - 1
        self.rest = [1 << k for k in range(total) if (1 << k) not in self.bits]
        me = lax.axis_index("batch").astype(jnp.int32)
        place = jnp.zeros((), jnp.int32)
        for k in order:
            place = place * 2 + ((me >> k) & 1)
        self.place = place

    def move(self, x, bit):
        return swap(x, "batch", self.size, bit)

    def __call__(self, keep, send, ties):
        ties = list(ties)

        def held(got):
            tie = ties.pop(0) if ties else None
            return got if tie is None else after(got, tie)

        got = held(self.move(send, self.bits[0]))
        for bit in self.bits[1:]:
            half = keep.shape[0] // 2
            now = keep.astype(F32) + got.astype(F32)
            keep, send = now[:half], now[half:].astype(BF)
            got = held(self.move(send, bit))
        piece = (keep + got.astype(F32)).astype(BF)
        for bit in self.rest:
            piece = (piece.astype(F32) + self.move(piece, bit).astype(F32)).astype(BF)
        for bit in self.bits[:0:-1]:
            piece = jnp.concatenate([piece, held(self.move(piece, bit))], axis=0)
        return piece, self.move(piece, self.bits[0])


def distance_of(row_ref):
    row = jnp.broadcast_to(row_ref[0].astype(F32), (row_ref.shape[2],) * 2)
    return row.T - row


def self_forward(tokens, gain, wq, wk, wv, rows, rel_bias, seqs, length, heads, groups):
    width = tokens.shape[1]
    total = (heads + 2 * groups) * HD
    share = heads // groups
    q_end, k_end = heads * HD, heads * HD + groups * HD

    def body(_, tok, g, wq_ref, wk_ref, wv_ref, row, rel, n1, qkv, probs, att):
        x = tok[...].astype(F32)
        normed = (x * rms_scale(x) * g[...]).astype(BF)
        n1[...] = normed
        qs, ks, vs = (dot(normed, w[...]).astype(BF) for w in (wq_ref, wk_ref, wv_ref))
        qkv[:, 0:q_end] = qs
        qkv[:, q_end:k_end] = ks
        qkv[:, k_end:total] = vs
        distance = distance_of(row)
        bias = [jnp.full((length, length), rel[h, 0], F32) for h in range(heads)]
        for level, bound in enumerate(BOUNDS, start=1):
            reached = distance >= bound
            bias = [jnp.where(reached, rel[h, level], bias[h]) for h in range(heads)]
        allowed = distance >= 0
        parts = []
        for h in range(heads):
            kv = h // share
            q = qs[:, h * HD : (h + 1) * HD]
            k = ks[:, kv * HD : (kv + 1) * HD]
            v = vs[:, kv * HD : (kv + 1) * HD]
            scores = jnp.where(allowed, dot(q, k, NT) * score_scale + bias[h], masked_score)
            weight = jnp.exp(scores - jnp.max(scores, axis=-1, keepdims=True))
            p = weight / jnp.sum(weight, axis=-1, keepdims=True)
            probs[0, h] = p
            parts.append(dot(p.astype(BF), v))
        att[...] = jnp.concatenate(parts, axis=-1).astype(BF)

    return call(
        body,
        (seqs,),
        jnp.zeros((1,), jnp.int32),
        [
            (tokens, (length, width), lambda s, *_: (s, 0)),
            (gain, (1, width), fixed(2)),
            whole(wq),
            whole(wk),
            whole(wv),
            (rows, (1, 1, length), lambda s, *_: (s, 0, 0)),
            (rel_bias, None, None),
        ],
        [
            ((seqs * length, width), BF, (length, width), lambda s, *_: (s, 0)),
            ((seqs * length, total), BF, (length, total), lambda s, *_: (s, 0)),
            (
                (seqs, heads, length, length),
                F32,
                (1, heads, length, length),
                lambda s, *_: (s, 0, 0, 0),
            ),
            ((seqs * length, heads * HD), BF, (length, heads * HD), lambda s, *_: (s, 0)),
        ],
        flops=2 * seqs * length * width * total,
        name="self_forward",
    )


def self_backward(qkv, probs, grad_att, rows, seqs, length, heads, groups):
    total = qkv.shape[1]
    share = heads // groups
    q_end, k_end = heads * HD, heads * HD + groups * HD
    edges = [-(1 << 30)] + BOUNDS + [1 << 30]

    def body(_, proj_ref, probs_ref, da, row, dqkv, grel):
        proj = proj_ref[...]
        distance = distance_of(row)
        grads_q, grads_k, grads_v, kept = [], [], [], []
        for h in range(heads):
            kv = h // share
            q = proj[:, h * HD : (h + 1) * HD]
            k = proj[:, q_end + kv * HD : q_end + (kv + 1) * HD]
            v = proj[:, k_end + kv * HD : k_end + (kv + 1) * HD]
            d = da[:, h * HD : (h + 1) * HD]
            p = probs_ref[0, h]
            dp = dot(d, v, NT)
            ds = (p * (dp - jnp.sum(dp * p, axis=-1, keepdims=True))).astype(BF)
            kept.append(ds.astype(F32))
            grads_q.append(dot(ds, k) * score_scale)
            dk = dot(ds, q, TN) * score_scale
            dv = dot(p.astype(BF), d, TN)
            if h % share:
                grads_k[kv] = grads_k[kv] + dk
                grads_v[kv] = grads_v[kv] + dv
            else:
                grads_k.append(dk)
                grads_v.append(dv)
        dqkv[...] = jnp.concatenate(grads_q + grads_k + grads_v, axis=-1).astype(BF)
        for level in range(NB):
            inside = jnp.logical_and(distance >= edges[level], distance < edges[level + 1])
            for h in range(heads):
                grel[0, level : level + 1, h * length : (h + 1) * length] = jnp.sum(
                    jnp.where(inside, kept[h], 0.0), axis=0, keepdims=True
                )

    return call(
        body,
        (seqs,),
        jnp.zeros((1,), jnp.int32),
        [
            (qkv, (length, total), lambda s, *_: (s, 0)),
            (probs, (1, heads, length, length), lambda s, *_: (s, 0, 0, 0)),
            (grad_att, (length, heads * HD), lambda s, *_: (s, 0)),
            (rows, (1, 1, length), lambda s, *_: (s, 0, 0)),
        ],
        [
            ((seqs * length, total), BF, (length, total), lambda s, *_: (s, 0)),
            (
                (seqs, NB, heads * length),
                F32,
                (1, NB, heads * length),
                lambda s, *_: (s, 0, 0),
            ),
        ],
        flops=10 * seqs * heads * length * length * HD,
        name="self_backward",
    )


def stack_heads(x, heads, groups):
    share = heads // groups
    zero = jnp.zeros((x.shape[0], HD), x.dtype)
    out = []
    for h in range(heads):
        own = x[:, h * HD : (h + 1) * HD]
        out.append(
            jnp.concatenate([own if g == h // share else zero for g in range(groups)], axis=-1)
        )
    return jnp.concatenate(out, axis=0)


def unstack_heads(x, heads, groups, length):
    share = heads // groups
    return jnp.concatenate(
        [
            x[(h // share) * HD : (h // share + 1) * HD, h * length : (h + 1) * length]
            for h in range(heads)
        ],
        axis=0,
    ).T


CHUNK = 256


def cross_forward(queries, kv, seqs, length, mem, heads, groups):
    wide = heads * length
    gw = groups * HD
    chunks = mem // CHUNK

    def body(_, q, kv_ref, att, lse, scores, acc):
        stacked = stack_heads(q[...], heads, groups) * jnp.asarray(score_scale, BF)

        def first(c, top):
            at = pl.ds(pl.multiple_of(c * CHUNK, CHUNK), CHUNK)
            s = dot(kv_ref[at, 0:gw], stacked, NT)
            scores[at, :] = s
            return jnp.maximum(top, jnp.max(s.reshape(CHUNK // 8, 8, wide), axis=0))

        top = lax.fori_loop(0, chunks, first, jnp.full((8, wide), -jnp.inf, F32))
        top = jnp.max(top, axis=0, keepdims=True)

        def second(c, total):
            at = pl.ds(pl.multiple_of(c * CHUNK, CHUNK), CHUNK)
            e = jnp.exp(scores[at, :] - top)
            scores[at, :] = e
            return total + jnp.sum(e.reshape(CHUNK // 8, 8, wide), axis=0)

        total = lax.fori_loop(0, chunks, second, jnp.zeros((8, wide), F32))
        total = jnp.sum(total, axis=0, keepdims=True)
        inverse = 1.0 / total
        lse[0] = top + jnp.log(total)
        acc[...] = jnp.zeros_like(acc)

        def third(c, carry):
            at = pl.ds(pl.multiple_of(c * CHUNK, CHUNK), CHUNK)
            p = (scores[at, :] * inverse).astype(BF)
            acc[...] += dot(kv_ref[at, gw : 2 * gw], p, TN)
            return carry

        lax.fori_loop(0, chunks, third, 0)
        att[...] = unstack_heads(acc[...], heads, groups, length).astype(BF)

    return call(
        body,
        (seqs,),
        jnp.zeros((1,), jnp.int32),
        [
            (queries, (length, heads * HD), lambda s, *_: (s, 0)),
            (kv, (mem, 2 * gw), lambda s, *_: (s, 0)),
        ],
        [
            ((seqs * length, heads * HD), BF, (length, heads * HD), lambda s, *_: (s, 0)),
            ((seqs, 1, wide), F32, (1, 1, wide), lambda s, *_: (s, 0, 0)),
        ],
        scratch=[pltpu.VMEM((mem, wide), F32), pltpu.VMEM((gw, wide), F32)],
        flops=8 * 4 * seqs * mem * wide * gw,
        name="cross_forward",
    )


def cross_backward(s, queries, kv, grad_att, lse, dq_so_far, seqs, length, mem, heads, groups):
    wide = heads * length
    gw = groups * HD
    chunks = mem // CHUNK

    def body(_, q, kv_ref, da, lse_ref, *refs):
        dq, dkv, probs, gprobs, acc = refs[-5:]
        stacked = stack_heads(q[...], heads, groups) * jnp.asarray(score_scale, BF)
        grads = stack_heads(da[...], heads, groups)
        level = lse_ref[0]

        def first(c, inner):
            at = pl.ds(pl.multiple_of(c * CHUNK, CHUNK), CHUNK)
            p = jnp.exp(dot(kv_ref[at, 0:gw], stacked, NT) - level)
            dp = dot(kv_ref[at, gw : 2 * gw], grads, NT)
            probs[at, :] = p
            gprobs[at, :] = dp
            dkv[at, gw : 2 * gw] = dot(p.astype(BF), grads).astype(BF)
            return inner + jnp.sum((p * dp).reshape(CHUNK // 8, 8, wide), axis=0)

        inner = lax.fori_loop(0, chunks, first, jnp.zeros((8, wide), F32))
        inner = jnp.sum(inner, axis=0, keepdims=True)
        acc[...] = jnp.zeros_like(acc)

        def second(c, carry):
            at = pl.ds(pl.multiple_of(c * CHUNK, CHUNK), CHUNK)
            ds = (probs[at, :] * (gprobs[at, :] - inner)).astype(BF)
            dkv[at, 0:gw] = dot(ds, stacked).astype(BF)
            acc[...] += dot(kv_ref[at, 0:gw], ds, TN)
            return carry

        lax.fori_loop(0, chunks, second, 0)
        dq[...] = (unstack_heads(acc[...], heads, groups, length) * score_scale).astype(BF)

    here = lambda *_: (s, 0)
    return call(
        body,
        (1,),
        jnp.zeros((1,), jnp.int32),
        [
            (queries, (length, heads * HD), here),
            (kv, (mem, 2 * gw), here),
            (grad_att, (length, heads * HD), here),
            (lse, (1, 1, wide), lambda *_: (s, 0, 0)),
        ],
        [
            ((seqs * length, heads * HD), BF, (length, heads * HD), here),
            ((mem, 2 * gw), BF, (mem, 2 * gw), fixed(2)),
        ],
        scratch=[
            pltpu.VMEM((mem, wide), F32),
            pltpu.VMEM((mem, wide), F32),
            pltpu.VMEM((gw, wide), F32),
        ],
        flops=8 * 10 * mem * wide * gw,
        name="cross_backward",
        onto=dq_so_far,
    )


TILE = 128


def joined(me, pieces, weights, acts, table):
    k = pieces[0].shape[1]

    @pl.when(pl.program_id(0) == 0)
    def _():
        for r, weight in enumerate(weights):
            table[pl.ds(pl.multiple_of((r ^ me) * k, k), k), :] = weight[...]

    for r, piece in enumerate(pieces):
        acts[:, pl.ds(pl.multiple_of((r ^ me) * k, k), k)] = piece[...]
    return dot(acts[...], table[...])


def join_ins(pieces, weights, part, tile):
    k, width = pieces[0].shape[1], weights[0].shape[1]
    return [(p, (tile, k), lambda i, *_: (i, 0)) for p in pieces] + [
        (w, (k, width), lambda *_: (part, 0)) for w in weights
    ]


def join_scratch(pieces, weights, tile):
    k, width = pieces[0].shape[1], weights[0].shape[1]
    return [pltpu.VMEM((tile, 4 * k), BF), pltpu.VMEM((4 * k, width), BF)]


def row_blocks(array):
    return (array, (TILE, array.shape[1]), lambda i, *_: (i, 0))


def whole(array):
    return (array, array.shape, fixed(array.ndim))


def out_rows(rows, cols, dtype):
    return ((rows, cols), dtype, (TILE, cols), lambda i, *_: (i, 0))


def join_self(me, pieces, weights, part, tokens, gain, wq):
    rows, width = tokens.shape
    k = pieces[0].shape[1]

    def body(me_ref, *refs):
        tok, g, wq_ref, x1, n2, q2, acts, table = refs[8:]
        x = tok[...].astype(F32) + joined(me_ref[0], refs[:4], refs[4:8], acts, table)
        x1[...] = x
        normed = (x * rms_scale(x) * g[...]).astype(BF)
        n2[...] = normed
        q2[...] = dot(normed, wq_ref[...]).astype(BF)

    return call(
        body,
        (rows // TILE,),
        me,
        join_ins(pieces, weights, part, TILE) + [row_blocks(tokens), whole(gain), whole(wq)],
        [
            out_rows(rows, width, F32),
            out_rows(rows, width, BF),
            out_rows(rows, wq.shape[1], BF),
        ],
        scratch=join_scratch(pieces, weights, TILE),
        flops=2 * rows * width * (4 * k + wq.shape[1]),
        name="join_self",
    )


def feed_forward(me, pieces, weights, part, x1, gain, gate_t, up_t, down, cot):
    rows, width = x1.shape
    k = pieces[0].shape[1]
    units = gate_t.shape[0]
    half = rows // 2
    per_half = half // TILE
    root = math.sqrt(2.0 / math.pi)

    def body(me_ref, *refs):
        x1_ref, g, wg, wu, wd, cot_ref, x2, n3, hid, dgate, dup, branch, dn3, acts, table = refs[8:]
        x = x1_ref[...] + joined(me_ref[0], refs[:4], refs[4:8], acts, table)
        x2[...] = x
        normed = (x * rms_scale(x) * g[...]).astype(BF)
        n3[...] = normed
        gate = dot(normed, wg[...], NT)
        up = dot(normed, wu[...], NT)
        square = gate * gate
        t = jnp.tanh(root * (gate + 0.044715 * (square * gate)))
        cdf = 0.5 * (1.0 + t)
        act = gate * cdf
        hidden = (act * up).astype(BF)
        hid[...] = hidden
        slope = cdf + 0.5 * gate * (1.0 - t * t) * (root * (1.0 + 3 * 0.044715 * square))
        dh = dot(cot_ref[...], wd[...], NT)
        dg = (dh * up * slope).astype(BF)
        du = (dh * act).astype(BF)
        dgate[...] = dg
        dup[...] = du
        dn3[0] = dot(dg, wg[...]) + dot(du, wu[...])
        branch[0] = dot(hidden, wd[...])

    def half_map(i, me_ref):
        return ((i // per_half) ^ (me_ref[0] & 1), i % per_half, 0)

    halves = ((2, half, width), F32, (1, TILE, width), half_map)
    return call(
        body,
        (rows // TILE,),
        me,
        join_ins(pieces, weights, part, TILE)
        + [
            row_blocks(x1),
            whole(gain),
            whole(gate_t),
            whole(up_t),
            whole(down),
            row_blocks(cot),
        ],
        [
            out_rows(rows, width, F32),
            out_rows(rows, width, BF),
            out_rows(rows, units, BF),
            out_rows(rows, units, BF),
            out_rows(rows, units, BF),
            halves,
            halves,
        ],
        scratch=join_scratch(pieces, weights, TILE),
        flops=2 * rows * width * (4 * k + 6 * units),
        name="feed_forward",
    )


def norm_pull(x, gain, dn, base):
    r = rms_scale(x)
    c = dn * gain
    grad = base + r * c - x * ((r * r * r) * jnp.mean(c * x, axis=-1, keepdims=True))
    return grad, jnp.sum(dn * x * r, axis=0, keepdims=True)


def accumulate(ref, value):
    @pl.when(pl.program_id(0) == 0)
    def _():
        ref[...] = value

    @pl.when(pl.program_id(0) > 0)
    def _():
        ref[...] += value


def gain_out(width):
    return ((1, width), F32, (1, width), fixed(2))


def half_blocks(array, per_half):
    return (array, (TILE, array.shape[1]), lambda i, *_: (i % per_half, 0))


def pull_ffn(me, own, other, x2, gain, cot, wout):
    rows, width = x2.shape
    per_half = own.shape[0] // TILE

    def body(me_ref, a, b, x_ref, g, cot_ref, w, dx, e, da, gn):
        mine = (pl.program_id(0) // per_half) == (me_ref[0] & 1)
        dn = jnp.where(mine, a[...], b[...])
        grad, gsum = norm_pull(x_ref[...], g[...], dn, cot_ref[...].astype(F32))
        dx[...] = grad
        low = grad.astype(BF)
        e[...] = low
        da[...] = dot(low, w[...], NT).astype(BF)
        accumulate(gn, gsum)

    return call(
        body,
        (rows // TILE,),
        me,
        [
            half_blocks(own, per_half),
            half_blocks(other, per_half),
            row_blocks(x2),
            whole(gain),
            row_blocks(cot),
            whole(wout),
        ],
        [
            out_rows(rows, width, F32),
            out_rows(rows, width, BF),
            out_rows(rows, wout.shape[0], BF),
            gain_out(width),
        ],
        flops=2 * rows * width * wout.shape[0],
        name="pull_ffn",
    )


def finish_layer(me, own, other, x2):
    rows, width = x2.shape
    per_half = own.shape[0] // TILE

    def body(me_ref, a, b, x_ref, out):
        mine = (pl.program_id(0) // per_half) == (me_ref[0] & 1)
        out[...] = x_ref[...] + jnp.where(mine, a[...], b[...])

    return call(
        body,
        (rows // TILE,),
        me,
        [half_blocks(own, per_half), half_blocks(other, per_half), row_blocks(x2)],
        [out_rows(rows, width, F32)],
        name="finish_layer",
    )[0]


def pull_cross(me, pieces, weights, part, x1, gain, base, wout):
    rows, width = x1.shape
    k = pieces[0].shape[1]

    def body(me_ref, *refs):
        x_ref, g, base_ref, wo, dx, e, da, gn, acts, table = refs[8:]
        dn = joined(me_ref[0], refs[:4], refs[4:8], acts, table)
        grad, gsum = norm_pull(x_ref[...], g[...], dn, base_ref[...])
        dx[...] = grad
        low = grad.astype(BF)
        e[...] = low
        da[...] = dot(low, wo[...], NT).astype(BF)
        accumulate(gn, gsum)

    return call(
        body,
        (rows // TILE,),
        me,
        join_ins(pieces, weights, part, TILE)
        + [row_blocks(x1), whole(gain), row_blocks(base), whole(wout)],
        [
            out_rows(rows, width, F32),
            out_rows(rows, width, BF),
            out_rows(rows, wout.shape[0], BF),
            gain_out(width),
        ],
        scratch=join_scratch(pieces, weights, TILE),
        flops=2 * rows * width * (4 * k + wout.shape[0]),
        name="pull_cross",
    )


def pull_self(me, pieces, weights, part, tokens, gain, base):
    rows, width = tokens.shape
    k = pieces[0].shape[1]

    def body(me_ref, *refs):
        x_ref, g, base_ref, dx, gn, acts, table = refs[8:]
        dn = joined(me_ref[0], refs[:4], refs[4:8], acts, table)
        grad, gsum = norm_pull(x_ref[...].astype(F32), g[...], dn, base_ref[...])
        dx[...] = grad
        accumulate(gn, gsum)

    return call(
        body,
        (rows // TILE,),
        me,
        join_ins(pieces, weights, part, TILE) + [row_blocks(tokens), whole(gain), row_blocks(base)],
        [out_rows(rows, width, F32), gain_out(width)],
        scratch=join_scratch(pieces, weights, TILE),
        flops=2 * rows * width * 4 * k,
        name="pull_self",
    )


def memory_grad(s, me, pieces, weights, part, seqs, so_far):
    rows, k = pieces[0].shape
    width = weights[0].shape[1]
    tile = 512
    steps = rows // tile

    def body(me_ref, *refs):
        out, acts, table = refs[-3:]
        out[...] = joined(me_ref[0], refs[:4], refs[4:8], acts, table).astype(BF)

    return call(
        body,
        (steps,),
        me,
        join_ins(pieces, weights, part, tile),
        [((seqs * rows, width), BF, (tile, width), lambda i, *_: (s * steps + i, 0))],
        scratch=join_scratch(pieces, weights, tile),
        flops=2 * rows * width * 4 * k,
        name="memory_grad",
        onto=so_far,
    )[0]


def pack_weights(out_cross, query_cross, key_cross, value_cross, wq, wk, wv):
    width = out_cross.shape[1]
    ins = (out_cross, query_cross, key_cross, value_cross, wq, wk, wv)

    def body(_, first, *refs):
        late, last = refs[-2:]
        start = first.shape[0]
        late[0:start, :] = first[...]
        for out, sources, at in ((late, refs[:3], start), (last, refs[3:6], 0)):
            for source in sources:
                high = source.shape[1]
                out[at : at + high, :] = source[...].T
                at += high

    one = out_cross.shape[0] + sum(w.shape[1] for w in ins[1:4])
    two = sum(w.shape[1] for w in ins[4:])
    return call(
        body,
        (1,),
        jnp.zeros((1,), jnp.int32),
        [whole(w) for w in ins],
        [
            ((one, width), BF, (one, width), fixed(2)),
            ((two, width), BF, (two, width), fixed(2)),
        ],
        name="pack_weights",
    )


def grad_feed(gate, up, hidden, n3, cot):
    rows, units = gate.shape
    width = n3.shape[1]
    part = width // 2

    def body(_, dg, du, h, n, c, out):
        out[0:units, :] = dot(dg[...], n[...], TN).astype(BF)
        out[units : 2 * units, :] = dot(du[...], n[...], TN).astype(BF)
        out[2 * units : 3 * units, :] = dot(h[...], c[...], TN).astype(BF)

    columns = lambda j, *_: (0, j)
    return call(
        body,
        (2,),
        jnp.zeros((1,), jnp.int32),
        [
            whole(gate),
            whole(up),
            whole(hidden),
            (n3, (rows, part), columns),
            (cot, (rows, part), columns),
        ],
        [((3 * units, width), BF, (3 * units, part), columns)],
        flops=6 * rows * units * width,
        name="grad_feed",
    )[0]


def put_blocks(places, store, parts):
    first, second = store
    at = [0, 0]
    for which, value in parts:
        high = value.shape[0]
        for j in range(BLOCKS):
            block = value[:, j * LANES : (j + 1) * LANES].astype(BF)
            store[which][j ^ places[which], at[which] : at[which] + high, :] = block
        at[which] += high


def block_outs(rows):
    half = BLOCKS // 2
    return [((half, r, LANES), BF, (half, r, LANES), fixed(3)) for r in rows for _ in range(2)]


def give_blocks(outs, store):
    half = BLOCKS // 2
    for n, blocks in enumerate(store):
        outs[2 * n][...] = blocks[0:half]
        outs[2 * n + 1][...] = blocks[half:BLOCKS]


def grad_self(places, dqkv, n1, a1, e1, q_width, k_width):
    rows, width = n1.shape
    high = (q_width + k_width, k_width + a1.shape[1])

    def body(place_ref, d, n, a, e, *refs):
        outs, store = refs[:4], refs[4:]
        at = (place_ref[0], place_ref[1])
        proj = dot(d[...], n[...], TN)
        put_blocks(
            at,
            store,
            [
                (0, proj[0 : q_width + k_width]),
                (1, proj[q_width + k_width :]),
                (1, dot(a[...], e[...], TN)),
            ],
        )
        give_blocks(outs, store)

    return call(
        body,
        (1,),
        places,
        [whole(dqkv), whole(n1), whole(a1), whole(e1)],
        block_outs(high),
        scratch=[pltpu.VMEM((BLOCKS, h, LANES), BF) for h in high],
        flops=2 * rows * width * sum(high),
        name="grad_self",
    )


def grad_cross(places, dkvs, memory, dq, n2, a2, e2, k_width):
    rows, width = memory.shape
    step = 1024
    per = dkvs[0].shape[0] // step
    count = len(dkvs)
    high = (dq.shape[1] + k_width, k_width + a2.shape[1])

    def body(place_ref, *refs):
        pieces, (mem_ref, d, n, a, e), rest = refs[:count], refs[count : count + 5], refs[count + 5 :]
        outs, store, lhs, acc = rest[:4], rest[4:6], rest[6], rest[7]
        i = pl.program_id(0)
        for s, piece in enumerate(pieces):

            @pl.when(i // per == s)
            def _(piece=piece):
                lhs[...] = piece[...]

        value = dot(lhs[...], mem_ref[...], TN)

        @pl.when(i == 0)
        def _():
            acc[...] = value

        @pl.when(i > 0)
        def _():
            acc[...] += value

        @pl.when(i == pl.num_programs(0) - 1)
        def _():
            put_blocks(
                (place_ref[0], place_ref[1]),
                store,
                [
                    (0, dot(d[...], n[...], TN)),
                    (0, acc[0:k_width, :]),
                    (1, acc[k_width : 2 * k_width, :]),
                    (1, dot(a[...], e[...], TN)),
                ],
            )
            give_blocks(outs, store)

    def piece_map(s):
        return lambda i, *_: (jnp.clip(i - s * per, 0, per - 1), 0)

    return call(
        body,
        (rows // step,),
        places,
        [(d, (step, d.shape[1]), piece_map(s)) for s, d in enumerate(dkvs)]
        + [(memory, (step, width), lambda i, *_: (i, 0))]
        + [whole(x) for x in (dq, n2, a2, e2)],
        block_outs(high),
        scratch=[pltpu.VMEM((BLOCKS, h, LANES), BF) for h in high]
        + [pltpu.VMEM((step, 2 * k_width), BF), pltpu.VMEM((2 * k_width, width), F32)],
        flops=2 * rows * width * 2 * k_width,
        name="grad_cross",
    )


def restore(places, first, second, q_width, k_width):
    half = first[0].shape[0]
    width = BLOCKS * LANES
    out_high = second[0].shape[1] - k_width

    def body(place_ref, lo0, hi0, lo1, hi1, q_out, k_out, v_out, o_out):
        for j in range(BLOCKS):
            blocks = []
            for n, (lo, hi) in enumerate(((lo0, hi0), (lo1, hi1))):
                at = j ^ place_ref[n]
                near = at & (half - 1)
                blocks.append(jnp.where(at < half, lo[near].astype(F32), hi[near].astype(F32)))
            here = slice(j * LANES, (j + 1) * LANES)
            q_out[here, :] = blocks[0][0:q_width].T
            k_out[here, :] = blocks[0][q_width : q_width + k_width].T
            v_out[here, :] = blocks[1][0:k_width].T
            o_out[:, here] = blocks[1][k_width:]

    def plain(rows, cols):
        return ((rows, cols), F32, (rows, cols), fixed(2))

    return call(
        body,
        (1,),
        places,
        [whole(x) for x in first + second],
        [
            plain(width, q_width),
            plain(width, k_width),
            plain(width, k_width),
            plain(out_high, width),
        ],
        name="restore",
    )


def on_device(
    group_size,
    batch_size,
    tokens,
    memory,
    positions,
    norm_self,
    query_self,
    key_self,
    value_self,
    out_self,
    rel_bias,
    norm_cross,
    query_cross,
    key_cross,
    value_cross,
    out_cross,
    norm_ffn,
    gate_in,
    up_in,
    down_proj,
    cotangent,
):
    seqs, length, width = tokens.shape
    mem = memory.shape[1]
    groups = key_self.shape[1] // HD
    heads = query_self.shape[1] // HD
    me = lax.axis_index("group").astype(jnp.int32)[None]
    along_y = BatchSum(batch_size, (0, 1, 2))
    along_z = BatchSum(batch_size, (1, 2, 0))
    places = jnp.stack([along_y.place, along_z.place])
    q_width, k_width = heads * HD, groups * HD

    tok = tokens.reshape(seqs * length, width)
    cot = cotangent.reshape(seqs * length, width)
    mem_rows = memory.reshape(seqs * mem, width)
    rows = positions[:, None, :]
    gain_self, gain_cross, gain_ffn = norm_self[None], norm_cross[None], norm_ffn[None]

    def gather(x):
        return gather_group(x, group_size)

    def sum_group(halves):
        got = swap(halves[1], "group", group_size, 1)
        mine = (halves[0] + got).astype(BF)
        full = mine.astype(F32) + swap(mine, "group", group_size, 2).astype(F32)
        return full, swap(full, "group", group_size, 1)

    all_out_self = gather(out_self)
    n1, qkv, probs, a1 = self_forward(
        tok, gain_self, query_self, key_self, value_self, rows, rel_bias.T,
        seqs, length, heads, groups,
    )
    a1_all = gather(a1)
    pack, pack_self = pack_weights(
        after(out_cross, a1), query_cross, key_cross, value_cross, query_self, key_self, value_self
    )
    kv = dot(mem_rows, pack[2 * q_width :], NT).astype(BF)
    all_pack = gather(after(pack, a1_all[2]))
    x1, n2, q2 = join_self(me, a1_all, all_out_self, 0, tok, gain_cross, query_cross)
    a2, lse = cross_forward(q2, kv, seqs, length, mem, heads, groups)
    a2_all = gather(a2)
    all_self = gather(after(pack_self, a2_all[2]))
    x2, n3, hidden, dgate, dup, branch, dn3 = feed_forward(
        me, a2_all, all_pack, 0, x1, gain_ffn, gate_in.T, up_in.T, down_proj, cot
    )

    dn3_own, dn3_other = sum_group(dn3)
    feed = grad_feed(dgate, dup, hidden, n3, cot)
    feed_sum = lax.psum(feed, "batch")
    dx2, e2, da2, gn_ffn = pull_ffn(
        me, dn3_own, dn3_other, after(x2, feed), gain_ffn, cot, out_cross
    )
    branch_own, branch_other = sum_group(after(branch, da2))
    dq2, dkvs = None, []
    for s in range(seqs):
        dq2, dkv = cross_backward(
            s, q2, kv, da2, lse, dq2, seqs, length, mem, heads, groups
        )
        dkvs.append(dkv)
    parts = [gather(dkvs[0])]
    dq2_all = gather(dq2)
    parts.append(gather(after(dkvs[1], dq2_all[2])))
    cross_blocks = grad_cross(places, dkvs, mem_rows, dq2, n2, a2, e2, k_width)
    dx1, e1, da1, gn_cross = pull_cross(
        me, dq2_all, all_pack, 1, after(x1, cross_blocks[0]), gain_cross, dx2, out_self
    )
    dqkv, grel = self_backward(qkv, probs, da1, rows, seqs, length, heads, groups)
    dqkv_all = gather(dqkv)
    for s in range(2, seqs):
        parts.append(gather(after(dkvs[s], dqkv_all[2])))
    self_blocks = grad_self(places, dqkv, n1, a1, e1, q_width, k_width)
    grad_tokens, gn_self = pull_self(
        me, dqkv_all, all_self, 0, tok, gain_self, after(dx1, self_blocks[0])
    )

    ties = (da1, dqkv, self_blocks[0], grad_tokens, None)
    cross_sums = (
        along_y(cross_blocks[0], cross_blocks[1], ties),
        along_z(cross_blocks[2], cross_blocks[3], ties),
    )
    ties = (grad_tokens,)
    self_sums = (
        along_y(self_blocks[0], self_blocks[1], ties),
        along_z(self_blocks[2], self_blocks[3], ties),
    )
    layer_out = finish_layer(me, branch_own, branch_other, after(x2, grad_tokens))

    grel = jnp.sum(grel.reshape(seqs, NB, heads, length), axis=(0, 3))
    small = jnp.concatenate([gn_self, gn_cross, gn_ffn, grel.reshape(1, -1)], axis=1)
    bit = 1
    while bit < batch_size:
        small = small + swap(small, "batch", batch_size, bit)
        bit *= 2

    grad_memory = None
    for s in range(seqs):
        grad_memory = memory_grad(
            s, me, parts[s], all_pack, 2, seqs, grad_memory
        )

    grad_query_cross, grad_key_cross, grad_value_cross, grad_out_cross = restore(
        places, *cross_sums, q_width, k_width
    )
    grad_query_self, grad_key_self, grad_value_self, grad_out_self = restore(
        places, *self_sums, q_width, k_width
    )
    units = down_proj.shape[0]
    grad_gate, grad_up, grad_down = (
        feed_sum[n * units : (n + 1) * units].astype(F32) for n in range(3)
    )

    flat = small[0]
    return (
        layer_out.reshape(seqs, length, width),
        grad_tokens.reshape(seqs, length, width),
        grad_memory.reshape(seqs, mem, width),
        flat[:width],
        grad_query_self,
        grad_key_self,
        grad_value_self,
        grad_out_self,
        flat[3 * width :].reshape(NB, heads),
        flat[width : 2 * width],
        grad_query_cross,
        grad_key_cross,
        grad_value_cross,
        grad_out_cross,
        flat[2 * width : 3 * width],
        grad_gate.T,
        grad_up.T,
        grad_down,
    )


def solution(mesh):
    placed = (
        P("batch", None, None),
        P("batch", None, None),
        P("batch", None),
        P(),
        P(None, "group"),
        P(None, "group"),
        P(None, "group"),
        P("group", None),
        P(None, "group"),
        P(),
        P(None, "group"),
        P(None, "group"),
        P(None, "group"),
        P("group", None),
        P(),
        P(None, "group"),
        P(None, "group"),
        P("group", None),
        P("batch", None, None),
    )
    group_size = mesh.shape["group"]
    batch_size = mesh.shape["batch"]

    def run(*args):
        return on_device(group_size, batch_size, *args)

    return jax.shard_map(
        run,
        mesh=mesh,
        in_specs=placed,
        out_specs=(
            P("batch", None, None),
            P("batch", None, None),
            P("batch", None, None),
            P(),
            P(None, "group"),
            P(None, "group"),
            P(None, "group"),
            P("group", None),
            P(None, "group"),
            P(),
            P(None, "group"),
            P(None, "group"),
            P(None, "group"),
            P("group", None),
            P(),
            P(None, "group"),
            P(None, "group"),
            P("group", None),
        ),
        check_vma=False,
    )
```
